32 devices in a mesh: replica: 4 (over z), table: 8 (over y, x, core).
Axes of the slice: x: 2, y: 2, z: 4, core: 2. Of those that a mesh axis runs over, the one named last changes fastest.
Arguments:
- table: float32 [8192, 128], P('table'), may hold values from -0.6 to 0.6
- row_state: float32 [8192], P('table'), may hold values from 4.7683717e-08 to 9.536743e-07
- lookup_grads: bfloat16 [4, 8192, 128], P('replica', 'table'), may hold values from -6 to 6
- lookup_slots: int32 [4, 8192], P('replica', 'table'), may hold values from 0 to 3
- lookup_rows: int32 [4, 8192], P('replica', 'table'), may hold values from 0 to 127
- block_ids: int32 [4, 32], P('replica', 'table'), may hold values from 0 to 7, as said below
- block_counts: int32 [4, 8], P('replica', 'table'), may hold values from 1 to 4, as said below
- inputs: bfloat16 [32768, 512], P(('replica', 'table')), may hold values from -509.11688 to 509.11688
- cotangent: bfloat16 [32768, 512], P(('replica', 'table')), may hold values from -45 to 45
- w_first: bfloat16 [512, 512], replicated, may hold values from -0.25 to 0.25
- w_second: bfloat16 [512, 512], replicated, may hold values from -0.25 to 0.25
Outputs:
- new_table: float32 [8192, 128], P('table')
- new_state: float32 [8192], P('table')
- new_first: bfloat16 [512, 512], replicated
- new_second: bfloat16 [512, 512], replicated
The draws below stay inside these ranges and needn't reach their ends.
Inputs may be any that keep to these rules, and one draw needn't show every extreme that they name: `block_ids`: within one device's 4 entries the block ids are distinct; entries of slots that are not live are not used. `block_counts`: some device uses all 4 slots in every draw.
All inputs are finite; a program needn't handle non-finite values.
Results may differ from the reference program's by a relative error of at most 0.00065.
The reference program's roundings to bfloat16 on the way (of `slot_grad`, `hidden` and `d_pre`) count: a program that leaves them out, or rounds other values in their place, can miss the bound.
Values may be sent and summed in bfloat16 or wider, within the bound.
No kernel may reach another device: no remote copies, remote signals or barrier semaphores. Data moves between devices by JAX's collectives and lax.ppermute only.
A program may use at most 64 MiB of HBM per device.

```python
import math
import jax
import jax.numpy as jnp
from jax import lax

EMB = 128
HID = 512
BLOCK_ROWS = 128
SLOTS = 4
BLOCKS_DEV = 8
LOOK_DEV = 1024
ROWS_DEV = 1024
TABLE_ROWS = 8192
ROWS = 32768
N_REPLICA = 4
N_TABLE = 8


def draw_block_ids(key, part):
    keys = jax.random.split(key, N_REPLICA * N_TABLE)

    def choose(sub_key):
        return jax.random.permutation(sub_key, BLOCKS_DEV)[:SLOTS]
    chosen = jax.vmap(choose)(keys)
    return chosen.astype(jnp.int32).reshape(N_REPLICA, N_TABLE * SLOTS)


def draw_block_counts(key, part):
    first_key, second_key = jax.random.split(jax.random.fold_in(key, 11))
    counts = jax.random.randint(first_key, (N_REPLICA * N_TABLE,), 1, SLOTS + 1)
    full_at = jax.random.randint(second_key, (), 0, N_REPLICA * N_TABLE)
    counts = counts.at[full_at].set(SLOTS)
    return counts.astype(jnp.int32).reshape(N_REPLICA, N_TABLE)


def scaled_rows(key, factor):
    keys = jax.random.split(key, 3)
    base = jax.random.normal(keys[0], (ROWS, HID), jnp.float32)
    base = jnp.clip(base, -5.0, 5.0)
    row_scale = jnp.exp(jax.random.uniform(keys[1], (ROWS, 1), jnp.float32, math.log(0.3), math.log(3.0)))
    col_scale = jnp.exp(jax.random.uniform(keys[2], (1, HID), jnp.float32, math.log(0.3), math.log(3.0)))
    return factor * base * row_scale * col_scale


def draw_inputs(key, part):
    values = scaled_rows(jax.random.fold_in(key, 21), 1.0)
    device_of_row = jnp.arange(ROWS, dtype=jnp.int32) // ROWS_DEV
    spike_col = device_of_row % HID
    heavy = (spike_col[:, None] == jnp.arange(HID, dtype=jnp.int32)[None, :]).astype(jnp.float32)
    boost = 2.0 * math.sqrt(min(N_REPLICA * N_TABLE, HID))
    return (values * (1.0 + (boost - 1.0) * heavy)).astype(jnp.bfloat16)


def draw_cotangent(key, part):
    factor = (LOOK_DEV * EMB / (HID * HID * ROWS_DEV)) ** 0.5 / 6.0
    return scaled_rows(jax.random.fold_in(key, 37), factor).astype(jnp.bfloat16)


def plant(drawn, stream_key, smallest, top_value):
    index_at = [jax.random.randint(jax.random.fold_in(stream_key, axis), (), 0, length) for axis, length in enumerate(drawn.shape)]
    main_axis = drawn.shape.index(max(drawn.shape))
    neighbour = index_at[:main_axis] + [(index_at[main_axis] + 1) % drawn.shape[main_axis]] + index_at[main_axis + 1:]
    return drawn.at[tuple(index_at)].set(smallest).at[tuple(neighbour)].set(top_value)


def block_scale(own_key, dims, cuts, least, high):
    def one(position, parts):
        draws = jax.random.uniform(jax.random.fold_in(jax.random.fold_in(own_key, 6), position), (parts,), jnp.float32, least / len(cuts), high / len(cuts))
        return jnp.repeat(jnp.exp(draws), dims[position] // parts).reshape((-1,) + (1,) * (len(dims) - position - 1))

    gain = one(*cuts[0])
    for cut in cuts[1:]:
        gain = gain * one(*cut)
    return gain


def scatter_about(own_key, shape, spread, reach, cuts=(), kind=jnp.bfloat16):
    drawn = spread * jax.random.normal(own_key, shape, jnp.float32)
    if cuts:
        drawn = drawn * block_scale(own_key, shape, cuts, -0.22, 0.18)
    return jnp.clip(drawn, -reach, reach).astype(kind)


def setup_inputs(seed: int = 0) -> dict:
    key_of = jax.random.split(jax.random.key(seed), 12)
    table = scatter_about(key_of[0], (TABLE_ROWS, EMB), 0.1, 0.6, ((0, 8),), jnp.float32)
    row_state = jnp.clip(jnp.exp(math.log(9.5367431640625e-07) - 2.9957323 * jax.random.uniform(key_of[1], (TABLE_ROWS,), jnp.float32) ** block_scale(key_of[1], (TABLE_ROWS,), ((0, 8),), -0.2, 0.2)), 4.7683716530855236e-08, 9.5367431640625e-07)
    lookup_grads = scatter_about(key_of[2], (N_REPLICA, N_TABLE * LOOK_DEV, EMB), 1.0, 6.0, ((0, 4), (1, 8)))
    lookup_slots = plant(jax.random.randint(key_of[3], (N_REPLICA, N_TABLE * LOOK_DEV), 0, SLOTS), jax.random.fold_in(key_of[3], 1), 0, SLOTS - 1).astype(jnp.int32)
    lookup_rows = plant(jax.random.randint(key_of[4], (N_REPLICA, N_TABLE * LOOK_DEV), 0, BLOCK_ROWS), jax.random.fold_in(key_of[4], 1), 0, BLOCK_ROWS - 1).astype(jnp.int32)
    block_ids = draw_block_ids(jax.random.fold_in(key_of[11], 71), 0)
    block_counts = draw_block_counts(jax.random.fold_in(key_of[11], 71), 0)
    inputs = draw_inputs(jax.random.fold_in(key_of[11], 71), 0)
    cotangent = draw_cotangent(jax.random.fold_in(key_of[11], 71), 0)
    w_first = scatter_about(key_of[9], (HID, HID), HID ** -0.5, 0.25)
    w_second = scatter_about(key_of[10], (HID, HID), HID ** -0.5, 0.25)
    return {"table": table, "row_state": row_state, "lookup_grads": lookup_grads, "lookup_slots": lookup_slots, "lookup_rows": lookup_rows, "block_ids": block_ids, "block_counts": block_counts, "inputs": inputs, "cotangent": cotangent, "w_first": w_first, "w_second": w_second}


def mlp_terms(inputs, cotangent, w_first, w_second):
    pre = jnp.dot(inputs, w_first, preferred_element_type=jnp.float32)
    sig = jax.nn.sigmoid(pre)
    hidden = (pre * sig).astype(jnp.bfloat16)
    back = jnp.dot(cotangent, w_second.T, preferred_element_type=jnp.float32)
    d_pre = (back * sig * (1.0 + pre * (1.0 - sig))).astype(jnp.bfloat16)
    grad_first = jnp.dot(inputs.T, d_pre, preferred_element_type=jnp.float32)
    grad_second = jnp.dot(hidden.T, cotangent, preferred_element_type=jnp.float32)
    return (grad_first, grad_second)

def reference(table, row_state, lookup_grads, lookup_slots, lookup_rows, block_ids, block_counts, inputs, cotangent, w_first, w_second):
    reps = N_REPLICA
    tabs = N_TABLE
    slot_ids = lookup_slots.reshape(reps, tabs, LOOK_DEV)
    row_ids = lookup_rows.reshape(reps, tabs, LOOK_DEV)
    live_look = (slot_ids < block_counts[:, :, None]).astype(jnp.float32)
    device_ids = (jnp.arange(reps, dtype=jnp.int32)[:, None] * tabs + jnp.arange(tabs, dtype=jnp.int32)[None, :]).astype(jnp.int32)
    flat_ids = ((device_ids[:, :, None] * SLOTS + slot_ids) * BLOCK_ROWS + row_ids).astype(jnp.int32).reshape(-1)
    grad_rows = lookup_grads.reshape(-1, EMB).astype(jnp.float32) * live_look.reshape(-1, 1)
    slot_grad = jax.ops.segment_sum(grad_rows, flat_ids, num_segments=reps * tabs * SLOTS * BLOCK_ROWS).astype(jnp.bfloat16)
    ids = block_ids.reshape(reps, tabs, SLOTS)
    live_slot = (jnp.arange(SLOTS, dtype=jnp.int32)[None, None, :] < block_counts[:, :, None]).astype(jnp.float32)
    dest_block = (jnp.arange(tabs, dtype=jnp.int32)[None, :, None] * BLOCKS_DEV + ids).astype(jnp.int32)
    dest = (dest_block[..., None] * BLOCK_ROWS + jnp.arange(BLOCK_ROWS, dtype=jnp.int32)).astype(jnp.int32).reshape(-1)
    weights = jnp.broadcast_to(live_slot[..., None], (reps, tabs, SLOTS, BLOCK_ROWS)).reshape(-1, 1)
    merged = jax.ops.segment_sum(slot_grad.astype(jnp.float32) * weights, dest, num_segments=tabs * BLOCKS_DEV * BLOCK_ROWS)
    xs = inputs.reshape(-1, ROWS_DEV, HID)
    ys = cotangent.reshape(-1, ROWS_DEV, HID)

    def step(carry, pair):
        first, second = mlp_terms(pair[0], pair[1], w_first, w_second)
        return ((carry[0] + first, carry[1] + second), None)
    zeros = jnp.zeros((HID, HID), jnp.float32)
    (grad_first, grad_second), _ = lax.scan(step, (zeros, zeros), (xs, ys))
    total = jnp.sum(merged * merged) + jnp.sum(grad_first * grad_first) + jnp.sum(grad_second * grad_second)
    clip_scale = jnp.minimum(1.0, 1.0 / (jnp.sqrt(total) + 1e-06))
    clipped = clip_scale * merged
    new_state = row_state + lax.optimization_barrier(jnp.mean(clipped * clipped, axis=1))
    new_table = table - 0.05 * clipped / jnp.sqrt(new_state)[:, None]
    rate = 0.04 * HID
    new_first = (w_first.astype(jnp.float32) - rate * clip_scale * grad_first).astype(jnp.bfloat16)
    new_second = (w_second.astype(jnp.float32) - rate * clip_scale * grad_second).astype(jnp.bfloat16)
    return (new_table, new_state, new_first, new_second)
```

```python
import functools

import jax
import jax.numpy as jnp
from jax import lax
from jax.experimental import pallas as pl
from jax.experimental.pallas import tpu as pltpu
from jax.sharding import PartitionSpec as P

BLOCK_ROWS = 128
LANES = 128
TILE = 8

emb_rate = 0.05
mlp_rate_unit = 0.04


f32 = jnp.float32
bf16 = jnp.bfloat16
VM = pl.BlockSpec(memory_space=pltpu.VMEM)
SM = pl.BlockSpec(memory_space=pltpu.SMEM)


def shape(dims, kind):
    return jax.ShapeDtypeStruct(dims, kind)


def call(body, out_shape, scalars, vectors, scratch=(), name=None, flops=0, moved=0):
    outs = jax.tree.map(lambda _: VM, out_shape)
    return pl.pallas_call(
        body,
        out_shape=out_shape,
        in_specs=[SM] * len(scalars) + [VM] * len(vectors),
        out_specs=outs,
        scratch_shapes=list(scratch),
        cost_estimate=pl.CostEstimate(flops=flops, bytes_accessed=moved, transcendentals=0),
        name=name,
    )(*scalars, *vectors)


def tree_sum(terms):
    while len(terms) > 1:
        terms = [terms[i] + terms[i + 1] for i in range(0, len(terms), 2)]
    return terms[0]


def slot_kernel(count_ref, ids_ref, slots_ref, rows_ref, grads_ref, out_ref, *, slot_count):
    live = count_ref[0, 0]
    slot = slots_ref[...]
    position = slot * BLOCK_ROWS + rows_ref[...]
    position = jnp.where(slot < live, position, -1)
    total = slot_count * BLOCK_ROWS
    targets = lax.broadcasted_iota(jnp.int32, (total, position.shape[1]), 0)
    onehot = jnp.where(targets == position, 1.0, 0.0).astype(bf16)
    summed = jnp.dot(onehot, grads_ref[0], preferred_element_type=f32)
    out_ref[pl.ds(0, total), :] = summed.astype(bf16)
    tail = out_ref.shape[0] - total
    row = lax.broadcasted_iota(jnp.int32, (tail, LANES), 0)
    marks = jnp.full((tail, LANES), -1, jnp.int32)
    for k in range(slot_count):
        block = jnp.where(k < live, ids_ref[0, k], -1)
        marks = jnp.where(row == k, block, marks)
    out_ref[pl.ds(total, tail), :] = marks.astype(f32).astype(bf16)


def merge_kernel(*refs, slot_count):
    parts, merged_ref, square_ref = refs[:-2], refs[-2], refs[-1]
    total = slot_count * BLOCK_ROWS
    marks = [p[pl.ds(total, 16), :].astype(f32) for p in parts]
    square = jnp.zeros((TILE, LANES), f32)
    for b in range(merged_ref.shape[0] // BLOCK_ROWS):
        terms = []
        for p, mark in zip(parts, marks):
            acc = jnp.zeros((BLOCK_ROWS, LANES), f32)
            for k in range(slot_count):
                hit = mark[k : k + 1, :] == float(b)
                data = p[pl.ds(k * BLOCK_ROWS, BLOCK_ROWS), :].astype(f32)
                acc = jnp.where(hit, data, acc)
            terms.append(acc)
        block = tree_sum(terms)
        merged_ref[pl.ds(b * BLOCK_ROWS, BLOCK_ROWS), :] = block
        square = square + jnp.sum((block * block).reshape(-1, TILE, LANES), axis=0)
    square_ref[...] = square


def across(a, b):
    return lax.dot_general(a, b, (((0,), (0,)), ((), ())), preferred_element_type=f32)


def mlp_kernel(
    where_ref, x_ref, c_ref, w1_ref, w2_ref, keep_ref, send_ref, h_ref, d_ref, *, cube
):
    half, me = where_ref[0], where_ref[1]
    rows, wide = x_ref.shape
    w1, w2 = w1_ref[...], w2_ref[...]
    step = min(256, rows)
    for r in range(rows // step):
        at = pl.ds(r * step, step)
        pre = jnp.dot(x_ref[at, :], w1, preferred_element_type=f32)
        sig = jax.nn.sigmoid(pre)
        h_ref[at, :] = (pre * sig).astype(bf16)
        back = lax.dot_general(
            c_ref[at, :], w2, (((1,), (1,)), ((), ())), preferred_element_type=f32
        )
        d_ref[at, :] = (back * sig * (1.0 + pre * (1.0 - sig))).astype(bf16)
    side = wide // 2
    piece = side // cube
    for out_ref, which in ((send_ref, 1 - half), (keep_ref, half)):
        at = pl.ds(pl.multiple_of(which * side, side), side)
        for m, grad in enumerate(
            (across(x_ref[:, at], d_ref[...]), across(h_ref[:, at], c_ref[...]))
        ):
            for q in range(cube):
                part = grad[q * piece : (q + 1) * piece, :]
                for col in range(wide // LANES):
                    out_ref[q ^ me, pl.ds((2 * col + m) * piece, piece), :] = part[
                        :, col * LANES : (col + 1) * LANES
                    ]


def add_kernel(a_ref, b_ref, *out_refs):
    for k, out_ref in enumerate(out_refs):
        out_ref[...] = a_ref[k] + b_ref[k]


def sum_kernel(*refs):
    total = refs[0][...]
    for ref in refs[1:-1]:
        total = total + ref[...]
    refs[-1][...] = total


def join_kernel(a_ref, b_ref, square_ref, out_ref):
    size = out_ref.shape[0] - TILE
    out_ref[pl.ds(0, size), :] = a_ref[pl.ds(0, size), :] + b_ref[pl.ds(0, size), :]
    out_ref[pl.ds(size, TILE), :] = square_ref[...]


def final_kernel(where_ref, *refs, cube, counted, rate):
    shares, refs = (refs[:cube], refs[cube : 2 * cube]), refs[2 * cube :]
    w1_ref, w2_ref, merged_ref, table_ref, state_ref = refs[:5]
    table_out, state_out, first_out, second_out = refs[5:]
    half, me = where_ref[0], where_ref[1]
    size = shares[0][0].shape[0] - TILE

    def square(ref):
        v = ref[pl.ds(0, size), :].reshape(-1, TILE, LANES)
        return jnp.sum(v * v, axis=0)

    mlp = tree_sum([tree_sum([square(ref) for ref in group]) for group in shares])
    emb = tree_sum(
        [tree_sum([group[k][pl.ds(size, TILE), :] for k in counted]) for group in shares]
    )
    total = jnp.sum(mlp + emb, axis=(0, 1), keepdims=True)
    clip = jnp.minimum(1.0, 1.0 / (jnp.sqrt(total) + 1e-06))
    scale = rate * clip
    wide = w1_ref.shape[0]
    side = wide // 2
    piece = side // cube
    for h, group in enumerate(shares):
        for k, ref in enumerate(group):
            base = (half ^ h) * side + (me ^ k) * piece
            at = pl.ds(pl.multiple_of(base, piece), piece)
            for m, (w_ref, out_ref) in enumerate(((w1_ref, first_out), (w2_ref, second_out))):
                grad = jnp.concatenate(
                    [ref[pl.ds((2 * c + m) * piece, piece), :] for c in range(wide // LANES)],
                    axis=1,
                )
                out_ref[at, :] = (w_ref[at, :].astype(f32) - scale * grad).astype(bf16)
    row = lax.broadcasted_iota(jnp.int32, (LANES, LANES), 0)
    col = lax.broadcasted_iota(jnp.int32, (LANES, LANES), 1)
    diagonal = row == col
    for b in range(table_ref.shape[0] // LANES):
        at = pl.ds(b * LANES, LANES)
        clipped = clip * merged_ref[at, :]
        mean = jnp.sum(clipped * clipped, axis=1, keepdims=True) * (1.0 / LANES)
        old = jnp.sum(jnp.where(diagonal, state_ref[b : b + 1, :], 0.0), axis=1, keepdims=True)
        fresh = old + mean
        table_out[at, :] = table_ref[at, :] - emb_rate * clipped / jnp.sqrt(fresh)
        state_out[b : b + 1, :] = jnp.sum(jnp.where(diagonal, fresh, 0.0), axis=0, keepdims=True)


def on_device(
    table,
    row_state,
    lookup_grads,
    lookup_slots,
    lookup_rows,
    block_ids,
    block_counts,
    inputs,
    cotangent,
    w_first,
    w_second,
    *,
    replicas,
    tables,
):
    slot_count = block_ids.shape[1]
    wide = w_first.shape[0]
    axes = ("replica", "table")

    def swap(value, mask):
        high, low = mask // tables, mask % tables
        if high == 0:
            pairs = [(i, i ^ low) for i in range(tables)]
            return lax.ppermute(value, "table", pairs)
        if low == 0:
            pairs = [(i, i ^ high) for i in range(replicas)]
            return lax.ppermute(value, "replica", pairs)
        pairs = [(i, i ^ mask) for i in range(replicas * tables)]
        return lax.ppermute(value, axes, pairs)

    bits = [1 << i for i in range((replicas * tables).bit_length() - 1)]
    pair = bits[0]
    cube_bits = [bits[1], bits[2], tables]
    rest = [b for b in bits[1:] if b not in cube_bits]
    cube = 1 << len(cube_bits)
    masks = [
        sum(bit for i, bit in enumerate(cube_bits) if k >> i & 1) for k in range(cube)
    ]
    flat = lax.axis_index(axes)
    half = (flat & pair) // pair
    me = sum(((flat & bit) // bit) << i for i, bit in enumerate(cube_bits))
    where = jnp.stack([half, me]).astype(jnp.int32)

    payload = call(
        functools.partial(slot_kernel, slot_count=slot_count),
        shape((slot_count * BLOCK_ROWS + 16, LANES), bf16),
        (block_counts, block_ids),
        (lookup_slots, lookup_rows, lookup_grads),
        name="slots",
        flops=2 * slot_count * BLOCK_ROWS * lookup_rows.shape[1] * LANES,
        moved=2 * lookup_grads.size,
    )
    payloads = [payload] + [swap(payload, k * tables) for k in range(1, replicas)]

    piece = wide // 2 // cube
    share = (2 * piece * wide // LANES, LANES)
    block = shape((cube,) + share, f32)
    keep, send = call(
        functools.partial(mlp_kernel, cube=cube),
        (block, block),
        (where,),
        (inputs, cotangent, w_first, w_second),
        scratch=[pltpu.VMEM(inputs.shape, bf16)] * 2,
        name="mlp",
        flops=8 * inputs.shape[0] * wide * wide,
        moved=4 * inputs.size + 16 * wide * wide,
    )
    other = swap(send, pair)
    parts = call(
        add_kernel, (shape(share, f32),) * cube, (), (keep, other), name="add",
        moved=12 * wide * wide,
    )
    received = [parts[0]] + [swap(parts[k], masks[k]) for k in range(1, cube)]
    total = call(
        sum_kernel, shape(share, f32), (), received, name="sum", moved=4 * wide * wide
    )
    merged, square = call(
        functools.partial(merge_kernel, slot_count=slot_count),
        (shape(table.shape, f32), shape((TILE, LANES), f32)),
        (),
        payloads,
        name="merge",
        flops=replicas * slot_count * table.size,
        moved=4 * table.size,
    )
    joined = shape((share[0] + TILE, LANES), f32)
    for bit in rest:
        if bit < tables:
            square = square + swap(square, bit)
    for bit in rest[:-1]:
        total = total + swap(total, bit)
    share_sum = call(
        join_kernel, joined, (), (total, swap(total, rest[-1]), square), name="join",
        moved=12 * share[0] * LANES,
    )
    own = [share_sum] + [swap(share_sum, masks[k]) for k in range(1, cube)]
    partner = [swap(v, pair) for v in own]
    counted = tuple(k for k in range(cube) if masks[k] < tables)
    table_shape = shape(table.shape, f32)
    state = row_state.reshape(-1, LANES)
    weight = shape(w_first.shape, bf16)
    new_table, new_state, new_first, new_second = call(
        functools.partial(
            final_kernel, cube=cube, counted=counted, rate=mlp_rate_unit * wide
        ),
        (table_shape, shape(state.shape, f32), weight, weight),
        (where,),
        (*own, *partner, w_first, w_second, merged, table, state),
        name="final",
        flops=8 * wide * wide,
        moved=16 * wide * wide + 12 * table.size,
    )
    return (new_table, new_state.reshape(-1), new_first, new_second)


def solution(mesh):
    placed = (
        P("table", None),
        P("table"),
        P("replica", "table", None),
        P("replica", "table"),
        P("replica", "table"),
        P("replica", "table"),
        P("replica", "table"),
        P(("replica", "table"), None),
        P(("replica", "table"), None),
        P(),
        P(),
    )
    return jax.shard_map(
        functools.partial(
            on_device, replicas=mesh.shape["replica"], tables=mesh.shape["table"]
        ),
        mesh=mesh,
        in_specs=placed,
        out_specs=(P("table", None), P("table"), P(), P()),
        check_vma=False,
    )
```

```python
import functools

import jax
import jax.numpy as jnp
from jax import lax
from jax.experimental import pallas as pl
from jax.experimental.pallas import tpu as pltpu
from jax.sharding import PartitionSpec as P


BLOCK_ROWS = 128
LANES = 128
TILE = 8

emb_rate = 0.05
mlp_rate_unit = 0.04


CUBE_ORDER = (7, 1, 6, 2, 5, 4, 3)

GATHER_ORDER = (6, 1, 5, 2, 3, 4, 7)


f32 = jnp.float32
bf16 = jnp.bfloat16
VM = pl.BlockSpec(memory_space=pltpu.VMEM)
SM = pl.BlockSpec(memory_space=pltpu.SMEM)
HBM = pl.BlockSpec(memory_space=pltpu.HBM)


def shape(dims, kind):
    return jax.ShapeDtypeStruct(dims, kind)


def call(body, out_shape, scalars, vectors, scratch=(), flops=0, moved=0, room=8, far=0):
    outs = jax.tree.map(lambda _: VM, out_shape)
    vectors = [
        pltpu.with_memory_space_constraint(v, pltpu.HBM) if i < far else v
        for i, v in enumerate(vectors)
    ]
    return pl.pallas_call(
        body,
        out_shape=out_shape,
        in_specs=[SM] * len(scalars) + [HBM] * far + [VM] * (len(vectors) - far),
        out_specs=outs,
        scratch_shapes=list(scratch),
        cost_estimate=pl.CostEstimate(flops=flops, bytes_accessed=moved, transcendentals=0),
        compiler_params=pltpu.CompilerParams(vmem_limit_bytes=room << 20),
    )(*scalars, *vectors)


def tree_sum(terms):
    while len(terms) > 1:
        terms = [terms[i] + terms[i + 1] for i in range(0, len(terms), 2)]
    return terms[0]


def fetch(pairs, sems):
    copies = [pltpu.make_async_copy(src, dst, sems.at[i]) for i, (src, dst) in enumerate(pairs)]
    for copy in copies:
        copy.start()
    return copies


def slot_kernel(*refs, slot_count):
    sources, count_ref, (out_ref, x_ref, c_ref, w1_ref, w2_ref) = refs[:8], refs[8], refs[9:14]
    ids_ref, slots_ref, rows_ref, grads_ref, sems = refs[14:]
    targets = (ids_ref, slots_ref, rows_ref, grads_ref, x_ref, c_ref, w1_ref, w2_ref)
    copies = fetch(zip(sources, targets), sems)
    live = count_ref[...]
    for copy in copies[:3]:
        copy.wait()
    slot = slots_ref[...]
    position = slot * BLOCK_ROWS + rows_ref[...]
    position = jnp.where(slot < live, position, -1)
    total = slot_count * BLOCK_ROWS
    targets = lax.broadcasted_iota(jnp.int32, (total, position.shape[1]), 0)
    onehot = jnp.where(targets == position, 1.0, 0.0).astype(bf16)
    copies[3].wait()
    summed = jnp.dot(onehot, grads_ref[0], preferred_element_type=f32)
    out_ref[pl.ds(0, total), :] = summed.astype(bf16)
    tail = out_ref.shape[0] - total
    row = lax.broadcasted_iota(jnp.int32, (tail, LANES), 0)
    marks = jnp.full((tail, LANES), -1, jnp.int32)
    for k in range(slot_count):
        block = jnp.where(live > k, ids_ref[:, k : k + 1], -1)
        marks = jnp.where(row == k, block, marks)
    out_ref[pl.ds(total, tail), :] = marks.astype(f32).astype(bf16)
    for copy in copies[4:]:
        copy.wait()


def merge_kernel(*refs, slot_count):
    parts, merged_ref, square_ref = refs[:-2], refs[-2], refs[-1]
    total = slot_count * BLOCK_ROWS
    marks = [p[pl.ds(total, 16), :].astype(f32) for p in parts]
    square = jnp.zeros((TILE, LANES), f32)
    for b in range(merged_ref.shape[0] // BLOCK_ROWS):
        terms = []
        for p, mark in zip(parts, marks):
            acc = jnp.zeros((BLOCK_ROWS, LANES), f32)
            for k in range(slot_count):
                hit = mark[k : k + 1, :] == float(b)
                data = p[pl.ds(k * BLOCK_ROWS, BLOCK_ROWS), :].astype(f32)
                acc = jnp.where(hit, data, acc)
            terms.append(acc)
        block = tree_sum(terms)
        merged_ref[pl.ds(b * BLOCK_ROWS, BLOCK_ROWS), :] = block
        square = square + jnp.sum((block * block).reshape(-1, TILE, LANES), axis=0)
    square_ref[...] = square


def across(a, b):
    return lax.dot_general(a, b, (((0,), (0,)), ((), ())), preferred_element_type=f32)


def put_shares(out_ref, m, grad, me, cube):
    piece = grad.shape[0] // cube
    for q in range(cube):
        part = grad[q * piece : (q + 1) * piece, :]
        for col in range(grad.shape[1] // LANES):
            out_ref[q ^ me, pl.ds((2 * col + m) * piece, piece), :] = part[
                :, col * LANES : (col + 1) * LANES
            ]


def side_of(which, wide):
    side = wide // 2
    return pl.ds(pl.multiple_of(which * side, side), side)


def send_kernel(where_ref, x_ref, c_ref, w1_ref, w2_ref, send_ref, h_ref, d_ref, *, cube):
    half, me = where_ref[0], where_ref[1]
    rows, wide = x_ref.shape
    w1, w2 = w1_ref[...], w2_ref[...]
    step = min(256, rows)
    for r in range(rows // step):
        at = pl.ds(r * step, step)
        pre = jnp.dot(x_ref[at, :], w1, preferred_element_type=f32)
        sig = jax.nn.sigmoid(pre)
        h_ref[at, :] = (pre * sig).astype(bf16)
        back = lax.dot_general(
            c_ref[at, :], w2, (((1,), (1,)), ((), ())), preferred_element_type=f32
        )
        d_ref[at, :] = (back * sig * (1.0 + pre * (1.0 - sig))).astype(bf16)
    at = side_of(1 - half, wide)
    put_shares(send_ref, 0, across(x_ref[:, at], d_ref[...]), me, cube)
    put_shares(send_ref, 1, across(h_ref[:, at], c_ref[...]), me, cube)


def keep_kernel(where_ref, x_ref, c_ref, h_ref, d_ref, keep_ref, *, cube):
    half, me = where_ref[0], where_ref[1]
    at = side_of(half, x_ref.shape[1])
    put_shares(keep_ref, 0, across(x_ref[:, at], d_ref[...]), me, cube)
    put_shares(keep_ref, 1, across(h_ref[:, at], c_ref[...]), me, cube)


def add_kernel(a_ref, b_ref, *out_refs):
    for k, out_ref in enumerate(out_refs):
        out_ref[...] = a_ref[k] + b_ref[k]


def sum_kernel(*refs):
    total = refs[0][...]
    for ref in refs[1:-1]:
        total = total + ref[...]
    refs[-1][...] = total


def join_kernel(a_ref, b_ref, square_ref, out_ref):
    size = out_ref.shape[0] - TILE
    out_ref[pl.ds(0, size), :] = a_ref[pl.ds(0, size), :] + b_ref[pl.ds(0, size), :]
    out_ref[pl.ds(size, TILE), :] = square_ref[...]


def final_kernel(where_ref, *refs, cube, counted, rate):
    shares, refs = (refs[:cube], refs[cube : 2 * cube]), refs[2 * cube :]
    w1_ref, w2_ref, merged_ref, table_ref, state_ref = refs[:5]
    table_out, state_out, first_out, second_out = refs[5:]
    half, me = where_ref[0], where_ref[1]
    size = shares[0][0].shape[0] - TILE

    def square(ref):
        v = ref[pl.ds(0, size), :].reshape(-1, TILE, LANES)
        return jnp.sum(v * v, axis=0)

    mlp = tree_sum([tree_sum([square(ref) for ref in group]) for group in shares])
    emb = tree_sum(
        [tree_sum([group[k][pl.ds(size, TILE), :] for k in counted]) for group in shares]
    )
    total = jnp.sum(mlp + emb, axis=(0, 1), keepdims=True)
    clip = jnp.minimum(1.0, 1.0 / (jnp.sqrt(total) + 1e-06))
    scale = rate * clip
    wide = w1_ref.shape[0]
    side = wide // 2
    piece = side // cube
    for h, group in enumerate(shares):
        for k, ref in enumerate(group):
            base = (half ^ h) * side + (me ^ k) * piece
            at = pl.ds(pl.multiple_of(base, piece), piece)
            for m, (w_ref, out_ref) in enumerate(((w1_ref, first_out), (w2_ref, second_out))):
                grad = jnp.concatenate(
                    [ref[pl.ds((2 * c + m) * piece, piece), :] for c in range(wide // LANES)],
                    axis=1,
                )
                out_ref[at, :] = (w_ref[at, :].astype(f32) - scale * grad).astype(bf16)
    row = lax.broadcasted_iota(jnp.int32, (LANES, LANES), 0)
    col = lax.broadcasted_iota(jnp.int32, (LANES, LANES), 1)
    diagonal = row == col
    for b in range(table_ref.shape[0] // LANES):
        at = pl.ds(b * LANES, LANES)
        clipped = clip * merged_ref[at, :]
        mean = jnp.sum(clipped * clipped, axis=1, keepdims=True) * (1.0 / LANES)
        old = jnp.sum(jnp.where(diagonal, state_ref[b : b + 1, :], 0.0), axis=1, keepdims=True)
        fresh = old + mean
        table_out[at, :] = table_ref[at, :] - emb_rate * clipped / jnp.sqrt(fresh)
        state_out[b : b + 1, :] = jnp.sum(jnp.where(diagonal, fresh, 0.0), axis=0, keepdims=True)


def on_device(
    table,
    row_state,
    lookup_grads,
    lookup_slots,
    lookup_rows,
    block_ids,
    block_counts,
    inputs,
    cotangent,
    w_first,
    w_second,
    *,
    replicas,
    tables,
):
    slot_count = block_ids.shape[1]
    wide = w_first.shape[0]
    axes = ("replica", "table")

    def swap(value, mask):
        high, low = mask // tables, mask % tables
        if high == 0:
            pairs = [(i, i ^ low) for i in range(tables)]
            return lax.ppermute(value, "table", pairs)
        if low == 0:
            pairs = [(i, i ^ high) for i in range(replicas)]
            return lax.ppermute(value, "replica", pairs)
        pairs = [(i, i ^ mask) for i in range(replicas * tables)]
        return lax.ppermute(value, axes, pairs)

    bits = [1 << i for i in range((replicas * tables).bit_length() - 1)]
    pair = bits[0]
    cube_bits = [bits[1], bits[2], tables]
    rest = [b for b in bits[1:] if b not in cube_bits]
    cube = 1 << len(cube_bits)
    masks = [
        sum(bit for i, bit in enumerate(cube_bits) if k >> i & 1) for k in range(cube)
    ]
    flat = lax.axis_index(axes)
    half = (flat & pair) // pair
    me = sum(((flat & bit) // bit) << i for i, bit in enumerate(cube_bits))
    where = jnp.stack([half, me]).astype(jnp.int32)

    lookups = (block_ids, lookup_slots, lookup_rows, lookup_grads)
    operands = (inputs, cotangent, w_first, w_second)
    payload, near_inputs, near_cotangent, near_first, near_second = call(
        functools.partial(slot_kernel, slot_count=slot_count),
        (shape((slot_count * BLOCK_ROWS + 16, LANES), bf16),)
        + tuple(shape(v.shape, v.dtype) for v in operands),
        (),
        lookups + operands + (block_counts,),
        far=len(lookups) + len(operands),
        scratch=[pltpu.VMEM(v.shape, v.dtype) for v in lookups]
        + [pltpu.SemaphoreType.DMA((len(lookups) + len(operands),))],
        flops=2 * slot_count * BLOCK_ROWS * lookup_rows.shape[1] * LANES,
        moved=2 * lookup_grads.size,
    )
    payloads = {0: payload}
    for bit in [1 << i for i in reversed(range(replicas.bit_length() - 1))]:
        for k in list(payloads):
            payloads[k ^ bit] = swap(payloads[k], bit * tables)
    payloads = [payloads[k] for k in range(replicas)]

    piece = wide // 2 // cube
    share = (2 * piece * wide // LANES, LANES)
    block = shape((cube,) + share, f32)
    middle = shape(inputs.shape, bf16)
    send, hidden, d_pre = call(
        functools.partial(send_kernel, cube=cube),
        (block, middle, middle),
        (where,),
        (near_inputs, near_cotangent, near_first, near_second),
        room=24,
        flops=6 * inputs.shape[0] * wide * wide,
        moved=4 * inputs.size + 16 * wide * wide,
    )
    other = swap(send, pair)
    keep = call(
        functools.partial(keep_kernel, cube=cube),
        block,
        (where,),
        (near_inputs, near_cotangent, hidden, d_pre),
        room=24,
        flops=2 * inputs.shape[0] * wide * wide,
        moved=4 * inputs.size + 16 * wide * wide,
    )
    parts = call(
        add_kernel, (shape(share, f32),) * cube, (), (keep, other),
        moved=12 * wide * wide,
    )
    received = [parts[0]] * cube
    for k in CUBE_ORDER:
        received[k] = swap(parts[k], masks[k])
    total = call(sum_kernel, shape(share, f32), (), received, moved=4 * wide * wide)
    merged, square = call(
        functools.partial(merge_kernel, slot_count=slot_count),
        (shape(table.shape, f32), shape((TILE, LANES), f32)),
        (),
        payloads,
        flops=replicas * slot_count * table.size,
        moved=4 * table.size,
    )
    joined = shape((share[0] + TILE, LANES), f32)
    for bit in rest:
        if bit < tables:
            square = square + swap(square, bit)
    for bit in rest[:-1]:
        total = total + swap(total, bit)
    last = swap(total, rest[-1])
    share_sum = call(
        join_kernel, joined, (), (total, last, square),
        moved=12 * share[0] * LANES,
    )
    own = [share_sum] * cube
    for k in GATHER_ORDER:
        own[k] = swap(share_sum, masks[k])
    partner = [swap(share_sum, pair)] * cube
    for k in GATHER_ORDER:
        partner[k] = swap(own[k], pair)
    counted = tuple(k for k in range(cube) if masks[k] < tables)
    table_shape = shape(table.shape, f32)
    state = row_state.reshape(-1, LANES)
    weight = shape(w_first.shape, bf16)
    new_table, new_state, new_first, new_second = call(
        functools.partial(
            final_kernel, cube=cube, counted=counted, rate=mlp_rate_unit * wide
        ),
        (table_shape, shape(state.shape, f32), weight, weight),
        (where,),
        (*own, *partner, near_first, near_second, merged, table, state),
        room=16,
        flops=8 * wide * wide,
        moved=16 * wide * wide + 12 * table.size,
    )
    return (new_table, new_state.reshape(-1), new_first, new_second)


def solution(mesh):
    placed = (
        P("table", None),
        P("table"),
        P("replica", "table", None),
        P("replica", "table"),
        P("replica", "table"),
        P("replica", "table"),
        P("replica", "table"),
        P(("replica", "table"), None),
        P(("replica", "table"), None),
        P(),
        P(),
    )

    def body(*args):
        return on_device(
            *args, replicas=mesh.shape["replica"], tables=mesh.shape["table"]
        )

    return jax.shard_map(
        body,
        mesh=mesh,
        in_specs=placed,
        out_specs=(P("table", None), P("table"), P(), P()),
        check_vma=False,
    )
```
